128 devices in a mesh: rep: 4 (over z_lo, core), shard: 32 (over y, z_hi, x).
Axes of the slice: x: 4, y: 4, z: 4 (z_hi: 2, z_lo: 2; z = z_hi * 2 + z_lo), core: 2. Of those that a mesh axis runs over, the one named last changes fastest.
Arguments:
- weight: bfloat16 [4, 32, 512, 2048], P('rep', None, 'shard'), may hold values from -3 to 3
- tracker: float32 [4, 32, 512, 2048], P('rep', None, 'shard'), may hold values from -40 to 40, as said below
- grad_new: bfloat16 [4, 32, 512, 2048], P('rep', None, 'shard'), may hold values from -6 to 6
- grad_old: bfloat16 [4, 32, 512, 2048], P('rep', None, 'shard'), may hold values from -6 to 6
- mix_keep: int32 [4, 2], replicated, may hold values from 4 to 12, as said below
Outputs:
- new_weight: bfloat16 [4, 32, 512, 2048], P('rep', None, 'shard')
- new_tracker: float32 [4, 32, 512, 2048], P('rep', None, 'shard')
- update: bfloat16 [4, 32, 512, 2048], P('rep', None, 'shard')
The draws below stay inside these ranges and needn't reach their ends.
Inputs may be any that keep to these rules, and one draw needn't show every extreme that they name: `mix_keep`: every entry is one of the integers 4 to 12; some entry equals 4 and some equals 12. `tracker`: finite real values.
All inputs are finite; a program needn't handle non-finite values.
Results may differ from the reference program's by a relative error of at most 0.023.
Values may be sent and summed in bfloat16 or wider, within the bound.
A program may use at most 128 MiB of HBM per device.

```python
import math
import jax
import jax.numpy as jnp
import numpy as np
from jax import lax

M = 512
N = 2048
NS_STEPS = 5
ROUNDS = 2
REPS = 4
EXPERTS = 32


def draw_tracker(key, part):
    key_noise, key_rows, key_cols = jax.random.split(key, 3)
    full_shape = (REPS, EXPERTS, M, N)
    log_low = math.log(0.3)
    log_high = math.log(3.0)
    base_noise = jnp.clip(jax.random.normal(key_noise, full_shape, jnp.float32), -4.0, 4.0)
    row_scale = jnp.exp(jax.random.uniform(key_rows, (REPS, EXPERTS, M, 1), jnp.float32, log_low, log_high))
    col_scale = jnp.exp(jax.random.uniform(key_cols, (REPS, EXPERTS, 1, N), jnp.float32, log_low, log_high))
    return base_noise * row_scale * col_scale


def draw_mix_keep(key, part):
    key_base, key_top, key_bottom = jax.random.split(key, 3)
    total_count = REPS * ROUNDS
    entries = jax.random.randint(key_base, (total_count,), 4, 13)
    top_pos = jax.random.randint(key_top, (), 0, total_count)
    bottom_pos = (top_pos + 1 + jax.random.randint(key_bottom, (), 0, total_count - 1)) % total_count
    entries = entries.at[top_pos].set(12).at[bottom_pos].set(4)
    return entries.reshape(REPS, ROUNDS).astype(jnp.int32)


def block_scale(stream_key, shape, shards, low, largest):
    def one(position, parts):
        draws = jax.random.uniform(jax.random.fold_in(jax.random.fold_in(stream_key, 6), position), (parts,), jnp.float32, low / len(shards), largest / len(shards))
        return jnp.repeat(jnp.exp(draws), shape[position] // parts).reshape((-1,) + (1,) * (len(shape) - position - 1))

    loudness = one(*shards[0])
    for cut in shards[1:]:
        loudness = loudness * one(*cut)
    return loudness


def scatter_about(stream_key, extent, width, bound, shards=(), held_as=jnp.bfloat16):
    array = jax.random.normal(stream_key, extent, jnp.float32) * width
    if len(shards) > 0:
        array = block_scale(stream_key, extent, shards, -0.22, 0.18) * array
    return jnp.clip(array, min=-bound, max=bound).astype(held_as)


def setup_inputs(seed: int = 0) -> dict:
    splits = jax.random.split(jax.random.key(seed), 6)
    return {
        "weight": scatter_about(splits[0], (REPS, EXPERTS, M, N), 0.5, 3.0, ((0, 4), (2, 32))),
        "tracker": draw_tracker(jax.random.fold_in(splits[5], 71), 0),
        "grad_new": scatter_about(splits[2], (REPS, EXPERTS, M, N), 1.0, 6.0, ((0, 4), (2, 32))),
        "grad_old": scatter_about(splits[3], (REPS, EXPERTS, M, N), 1.0, 6.0, ((0, 4), (2, 32))),
        "mix_keep": draw_mix_keep(jax.random.fold_in(splits[5], 71), 0),
    }


coeff_a = 3.4445
coeff_b = -4.775
coeff_c = 2.0315
learn_rate = 0.05

def orthogonalize(matrix):
    update_scale = 0.2 * math.sqrt(max(M, N))
    values = matrix.astype(jnp.float32)
    frob_norm = jnp.sqrt(jnp.sum(values * values))
    iterate = (values / (frob_norm + 1e-07)).astype(jnp.bfloat16)
    for iteration in range(NS_STEPS):
        gram_matrix = jnp.dot(iterate, iterate.T, preferred_element_type=jnp.float32).astype(jnp.bfloat16)
        square = jnp.dot(gram_matrix, gram_matrix, preferred_element_type=jnp.float32)
        polynomial = (coeff_b * gram_matrix.astype(jnp.float32) + coeff_c * square).astype(jnp.bfloat16)
        product = jnp.dot(polynomial, iterate, preferred_element_type=jnp.float32)
        iterate = (coeff_a * iterate.astype(jnp.float32) + product).astype(jnp.bfloat16)
    return (update_scale * iterate.astype(jnp.float32)).astype(jnp.bfloat16)

def reference(weight, tracker, grad_new, grad_old, mix_keep):
    replica_ids = np.arange(REPS)
    mixed_w = weight
    mixed_y = tracker
    for round_index in range(ROUNDS):
        partner_rows = replica_ids ^ 1 << round_index
        keep_column = mix_keep[:, round_index].astype(jnp.float32)
        own_share = (keep_column / 16.0)[:, None, None, None]
        other_share = ((16.0 - keep_column) / 16.0)[:, None, None, None]
        mixed_w = (own_share * mixed_w.astype(jnp.float32) + other_share * mixed_w[partner_rows].astype(jnp.float32)).astype(jnp.bfloat16)
        mixed_y = own_share * mixed_y + other_share * mixed_y[partner_rows]
    new_tracker = mixed_y + grad_new.astype(jnp.float32) - grad_old.astype(jnp.float32)
    rounded = lax.optimization_barrier(new_tracker.astype(jnp.bfloat16))
    matrices = rounded.reshape(REPS * EXPERTS, M, N)
    update = lax.map(orthogonalize, matrices).reshape(REPS, EXPERTS, M, N)
    new_weight = (mixed_w.astype(jnp.float32) - learn_rate * update.astype(jnp.float32)).astype(jnp.bfloat16)
    return (new_weight, new_tracker, update)
```

```python
import math

import jax
import jax.numpy as jnp
from jax import lax
from jax.sharding import PartitionSpec as P

NS_STEPS = 5


coeff_a = 3.4445
coeff_b = -4.775
coeff_c = 2.0315
learn_rate = 0.05


def swapped(shard, axis, bit):
    return lax.ppermute(shard, axis, [(i, i ^ 1 << bit) for i in range(lax.axis_size(axis))])


def gossip_weight(values, keep_row):
    for bit_index in range(keep_row.shape[0]):
        partner = swapped(values, "rep", bit_index)
        own_share = keep_row[bit_index] / 16.0
        other_share = (16.0 - keep_row[bit_index]) / 16.0
        values = (
            own_share * values.astype(jnp.float32) + other_share * partner.astype(jnp.float32)
        ).astype(jnp.bfloat16)
    return values


def gossip_tracker(values, keep_row):
    for bit_index in range(keep_row.shape[0]):
        partner = swapped(values.astype(jnp.bfloat16), "rep", bit_index).astype(values.dtype)
        own_share = keep_row[bit_index] / 16.0
        other_share = (16.0 - keep_row[bit_index]) / 16.0
        values = own_share * values + other_share * partner
    return values


def orthogonalize(block_in):
    update_scale = 0.2 * math.sqrt(max(block_in.shape[1], block_in.shape[2]))
    values = block_in.astype(jnp.float32)
    frob_norm = jnp.sqrt(jnp.sum(values * values, axis=(1, 2), keepdims=True))
    iterate = (values / (frob_norm + 1e-07)).astype(jnp.bfloat16)
    for iteration in range(NS_STEPS):
        gram_matrix = jnp.einsum(
            "kmn,kpn->kmp", iterate, iterate, preferred_element_type=jnp.float32
        ).astype(jnp.bfloat16)
        square = jnp.einsum(
            "kmp,kpq->kmq", gram_matrix, gram_matrix, preferred_element_type=jnp.float32
        )
        polynomial = (coeff_b * gram_matrix.astype(jnp.float32) + coeff_c * square).astype(
            jnp.bfloat16
        )
        product = jnp.einsum(
            "kmp,kpn->kmn", polynomial, iterate, preferred_element_type=jnp.float32
        )
        iterate = (coeff_a * iterate.astype(jnp.float32) + product).astype(jnp.bfloat16)
    return (update_scale * iterate.astype(jnp.float32)).astype(jnp.bfloat16)


def settle(block_in):
    update_block = orthogonalize(block_in[0])[None]
    shards = lax.axis_size("shard")
    rows = update_block.shape[2] // shards
    cut = update_block.reshape(shards, update_block.shape[1], rows, update_block.shape[3])
    return lax.all_to_all(cut, "shard", split_axis=0, concat_axis=0, tiled=True)


def local(weight, tracker, grad_new, grad_old, mix_keep):
    rep_index = lax.axis_index("rep")
    keep_all = mix_keep.astype(jnp.float32)
    keep_row = keep_all[rep_index]
    mixed_w = gossip_weight(weight, keep_row)
    mixed_y = gossip_tracker(tracker, keep_row)
    new_tracker = mixed_y + grad_new.astype(jnp.float32) - grad_old.astype(jnp.float32)
    rounded = new_tracker.astype(jnp.bfloat16)
    shards = lax.axis_size("shard")
    experts = rounded.shape[1]
    packed = rounded.reshape(shards, experts // shards, rounded.shape[2], rounded.shape[3])
    returned = settle(lax.all_to_all(packed, "shard", split_axis=0, concat_axis=2, tiled=True))
    update = returned.reshape(rounded.shape)
    new_weight = (mixed_w.astype(jnp.float32) - learn_rate * update.astype(jnp.float32)).astype(
        jnp.bfloat16
    )
    return (new_weight, new_tracker, update)


def solution(mesh):
    return jax.shard_map(
        local,
        mesh=mesh,
        in_specs=(
            P("rep", None, "shard", None),
            P("rep", None, "shard", None),
            P("rep", None, "shard", None),
            P("rep", None, "shard", None),
            P(),
        ),
        out_specs=(
            P("rep", None, "shard", None),
            P("rep", None, "shard", None),
            P("rep", None, "shard", None),
        ),
        check_vma=False,
    )
```

```python
import functools
import math

import jax
import jax.numpy as jnp
from jax import lax
from jax.experimental import pallas as pl
from jax.experimental.pallas import tpu as pltpu
from jax.sharding import PartitionSpec as P

MESH = pl.DeviceIdType.MESH
NS_STEPS = 5

coeff_a = 3.4445
coeff_b = -4.775
coeff_c = 2.0315
learn_rate = 0.05

X_SIZE, Z_SIZE = 4, 2
STRIDE = 13
LAG = 8


def peer_at(me, step, shards):
    y_size = shards // (X_SIZE * Z_SIZE)
    offset = lax.rem(step * STRIDE, shards)
    x = lax.rem(lax.rem(me, X_SIZE) + lax.rem(offset, X_SIZE), X_SIZE)
    z = lax.rem(lax.rem(lax.div(me, X_SIZE), Z_SIZE) + lax.rem(lax.div(offset, X_SIZE), Z_SIZE), Z_SIZE)
    y = lax.rem(lax.div(me, X_SIZE * Z_SIZE) + lax.div(offset, X_SIZE * Z_SIZE), y_size)
    return (y * Z_SIZE + z) * X_SIZE + x


def greet(rep, me, shards, others):
    barrier = pltpu.get_barrier_semaphore()

    @pl.loop(1, shards)
    def _(step):
        pl.semaphore_signal(barrier, inc=1, device_id=(rep, peer_at(me, step, shards)), device_id_type=MESH)

    for other in others:
        pl.semaphore_signal(barrier, inc=1, device_id=(other, me), device_id_type=MESH)
    return lambda: pl.semaphore_wait(barrier, shards - 1 + len(others))


def shares(keep, rep, bit):
    own = keep[rep, bit].astype(jnp.float32) / 16.0
    return own, 1.0 - own


def gossip_kernel(
    shards, keep, y, gn, go, w, x_out, nt, w1_out,
    yv, yb, yp, ub, up, gnv, gov, gs, wv, wp, w1v,
    y_sem, yb_send, yb_recv, u_send, u_recv, g_send, g_recv, nt_sem, in_sem, w_send, w_recv,
):
    rep, me = lax.axis_index("rep"), lax.axis_index("shard")
    core = rep + 1 - 2 * lax.rem(rep, 2)
    side = lax.rem(rep + 2, 4)
    enter = greet(rep, me, shards, (core, side))
    at = lambda step: peer_at(me, step, shards)

    def load_y(step):
        return pltpu.make_async_copy(y.at[at(step)], yv.at[at(step)], y_sem.at[step])

    def send_y(step):
        e = at(step)
        return pltpu.make_async_remote_copy(
            yb.at[e], yp.at[e], yb_send.at[step], yb_recv.at[step], device_id=(core, me), device_id_type=MESH
        )

    def send_u(step):
        e = at(step)
        return pltpu.make_async_remote_copy(
            ub.at[e], up.at[e], u_send.at[step], u_recv.at[step], device_id=(side, me), device_id_type=MESH
        )

    def send_g(step):
        e = at(step)
        return pltpu.make_async_remote_copy(
            gs.at[e], x_out.at[me], g_send.at[step], g_recv.at[step], device_id=(rep, e), device_id_type=MESH
        )

    def store_nt(step):
        e = at(step)
        return pltpu.make_async_copy(yv.at[e], nt.at[e], nt_sem.at[step])

    own_block = pltpu.make_async_copy(gs.at[me], x_out.at[me], g_recv.at[0])
    load_gn = pltpu.make_async_copy(gn, gnv, in_sem.at[0])
    load_go = pltpu.make_async_copy(go, gov, in_sem.at[1])
    load_w = pltpu.make_async_copy(w, wv, in_sem.at[2])
    store_w1 = pltpu.make_async_copy(w1v, w1_out, in_sem.at[3])
    send_w = pltpu.make_async_remote_copy(wv, wp, w_send, w_recv, device_id=(core, me), device_id_type=MESH)

    @pl.loop(0, shards)
    def _(step):
        load_y(step).start()

    load_gn.start()
    load_go.start()
    load_w.start()
    own0, other0 = shares(keep, rep, 0)
    own1, other1 = shares(keep, rep, 1)
    enter()

    @pl.loop(0, shards + LAG + 1)
    def _(tick):
        @pl.when(tick < shards)
        def _():
            load_y(tick).wait()
            e = at(tick)
            yb[e] = yv[e].astype(jnp.bfloat16)

        @pl.when((tick >= 1) & (tick <= shards))
        def _():
            send_y(tick - 1).start()

        @pl.when((tick >= LAG) & (tick < shards + LAG))
        def _():
            send_y(tick - LAG).wait_recv()
            e = at(tick - LAG)
            mixed = own0 * yv[e] + other0 * yp[e].astype(jnp.float32)
            yv[e] = mixed
            ub[e] = mixed.astype(jnp.bfloat16)

        @pl.when(tick >= LAG + 1)
        def _():
            send_u(tick - LAG - 1).start()

    load_w.wait()
    send_w.start()
    load_gn.wait()
    load_go.wait()

    @pl.loop(0, shards + 1)
    def _(tick):
        @pl.when(tick < shards)
        def _():
            send_u(tick).wait_recv()
            e = at(tick)
            fresh = (
                own1 * yv[e] + other1 * up[e].astype(jnp.float32)
                + gnv[e].astype(jnp.float32) - gov[e].astype(jnp.float32)
            )
            yv[e] = fresh
            gs[e] = fresh.astype(jnp.bfloat16)

        @pl.when(tick >= 2)
        def _():
            send_g(tick - 1).start()

        @pl.when(tick == 1)
        def _():
            own_block.start()

        @pl.when(tick >= 1)
        def _():
            store_nt(tick - 1).start()

    send_w.wait()

    @pl.loop(0, shards)
    def _(e):
        w1v[e] = (own0 * wv[e].astype(jnp.float32) + other0 * wp[e].astype(jnp.float32)).astype(jnp.bfloat16)

    store_w1.start()
    own_block.wait()

    @pl.loop(0, shards)
    def _(step):
        send_y(step).wait_send()
        send_u(step).wait_send()
        store_nt(step).wait()

    store_w1.wait()

    @pl.loop(1, shards)
    def _(step):
        send_g(step).wait()


def return_kernel(shards, us, ur, own, send, recv, sem):
    rep, me = lax.axis_index("rep"), lax.axis_index("shard")
    enter = greet(rep, me, shards, ())
    fetch = pltpu.make_async_copy(us.at[me], own, sem.at[0])
    put = pltpu.make_async_copy(own, ur.at[me], sem.at[1])
    fetch.start()

    def send_block(step):
        e = peer_at(me, step, shards)
        return pltpu.make_async_remote_copy(
            us.at[e], ur.at[me], send.at[step], recv.at[step], device_id=(rep, e), device_id_type=MESH
        )

    enter()

    @pl.loop(1, shards)
    def _(step):
        send_block(step).start()

    fetch.wait()
    put.start()
    put.wait()

    @pl.loop(1, shards)
    def _(step):
        send_block(step).wait()


def finish_kernel(keep, w1, w1p, ur, new_weight, update):
    own1, other1 = shares(keep, lax.axis_index("rep"), 1)
    mixed = (own1 * w1[...].astype(jnp.float32) + other1 * w1p[...].astype(jnp.float32)).astype(jnp.bfloat16)
    new_weight[...] = (mixed.astype(jnp.float32) - learn_rate * ur[...].astype(jnp.float32)).astype(jnp.bfloat16)
    update[...] = ur[...]


def orthogonalize(block_in):
    update_scale = 0.2 * math.sqrt(max(block_in.shape[0], block_in.shape[1]))
    values = block_in.astype(jnp.float32)
    frob_norm = jnp.sqrt(jnp.sum(values * values))
    iterate = (values / (frob_norm + 1e-07)).astype(jnp.bfloat16)
    for iteration in range(NS_STEPS):
        gram_matrix = jnp.einsum("mn,pn->mp", iterate, iterate, preferred_element_type=jnp.float32).astype(jnp.bfloat16)
        square = jnp.einsum("mp,pq->mq", gram_matrix, gram_matrix, preferred_element_type=jnp.float32)
        polynomial = (coeff_b * gram_matrix.astype(jnp.float32) + coeff_c * square).astype(jnp.bfloat16)
        product = jnp.einsum("mp,pn->mn", polynomial, iterate, preferred_element_type=jnp.float32)
        iterate = (coeff_a * iterate.astype(jnp.float32) + product).astype(jnp.bfloat16)
    return (update_scale * iterate.astype(jnp.float32)).astype(jnp.bfloat16)


def local(weight, tracker, grad_new, grad_old, mix_keep):
    shards = lax.axis_size("shard")
    block = weight.shape[1:]
    experts, rows, columns = block
    half = jax.ShapeDtypeStruct(block, jnp.bfloat16)
    full = jax.ShapeDtypeStruct(block, jnp.float32)
    anywhere = pl.BlockSpec(memory_space=pl.ANY)
    scalars = pl.BlockSpec(memory_space=pltpu.SMEM)
    vmem_half = pltpu.VMEM(block, jnp.bfloat16)
    dma = pltpu.SemaphoreType.DMA

    x, new_tracker, w1 = pl.pallas_call(
        functools.partial(gossip_kernel, shards),
        out_shape=(half, full, half),
        in_specs=[scalars] + [anywhere] * 4,
        out_specs=(anywhere,) * 3,
        scratch_shapes=[pltpu.VMEM(block, jnp.float32)] + [vmem_half] * 10
        + [dma((shards,))] * 8 + [dma((4,)), dma, dma],
        compiler_params=pltpu.CompilerParams(collective_id=0, has_side_effects=True, vmem_limit_bytes=48 << 20),
        name="gossip",
    )(mix_keep, tracker[0], grad_new[0], grad_old[0], weight[0])

    w1p = lax.ppermute(w1, "rep", [(i, i ^ 2) for i in range(lax.axis_size("rep"))])
    cut = orthogonalize(x.reshape(shards * rows, columns)).reshape(block)

    returned = pl.pallas_call(
        functools.partial(return_kernel, shards),
        out_shape=half,
        in_specs=[anywhere],
        out_specs=anywhere,
        scratch_shapes=[pltpu.VMEM((rows, columns), jnp.bfloat16), dma((shards,)), dma((shards,)), dma((2,))],
        compiler_params=pltpu.CompilerParams(collective_id=1, has_side_effects=True, vmem_limit_bytes=48 << 20),
        cost_estimate=pl.CostEstimate(flops=0, bytes_accessed=100 << 20, transcendentals=0),
        name="giveback",
    )(cut)

    step = 4
    tile = pl.BlockSpec((step, rows, columns), lambda i: (i, 0, 0))
    new_weight, update = pl.pallas_call(
        finish_kernel,
        grid=(experts // step,),
        out_shape=(half, half),
        in_specs=[scalars] + [tile] * 3,
        out_specs=(tile, tile),
        name="finish",
    )(mix_keep, w1, w1p, returned)
    return (new_weight[None], new_tracker[None], update[None])


def solution(mesh):
    spec = P("rep", None, "shard", None)
    return jax.shard_map(
        local,
        mesh=mesh,
        in_specs=(spec, spec, spec, spec, P()),
        out_specs=(spec, spec, spec),
        check_vma=False,
    )
```

```python
import functools
import math

import jax
import jax.numpy as jnp
from jax import lax
from jax.experimental import pallas as pl
from jax.experimental.pallas import tpu as pltpu
from jax.sharding import PartitionSpec as P

MESH = pl.DeviceIdType.MESH
NS_STEPS = 5

coeff_a = 3.4445
coeff_b = -4.775
coeff_c = 2.0315
learn_rate = 0.05

STRIDE = 13
HEAD = 8
LAG = 14


def peer_at(me, step, shards):
    return lax.bitwise_xor(me, lax.bitwise_and(step * STRIDE, shards - 1))


LINES = ((1, 2, 3), (8, 16, 24), (4,))


def greet(rep, me, others):
    barrier = pltpu.get_barrier_semaphore()
    near = [(rep, lax.bitwise_xor(me, bits)) for line in LINES for bits in line] + [(other, me) for other in others]
    for device in near:
        pl.semaphore_signal(barrier, inc=1, device_id=device, device_id_type=MESH)
    return lambda: pl.semaphore_wait(barrier, len(near))


def relay(rep, me, line, heard):
    for bits in line:
        pl.semaphore_signal(heard, inc=1, device_id=(rep, lax.bitwise_xor(me, bits)), device_id_type=MESH)
    return lambda: pl.semaphore_wait(heard, len(line))


def shares(keep, rep, bit):
    own = keep[bit, rep].astype(jnp.float32) / 16.0
    return own, 1.0 - own


def dot_nt(a, b):
    return lax.dot_general(a, b, (((1,), (1,)), ((), ())), preferred_element_type=jnp.float32)


def dot_nn(a, b):
    return lax.dot_general(a, b, (((1,), (0,)), ((), ())), preferred_element_type=jnp.float32)


def newton_schulz(x, gram, poly, total):
    size, width = x.shape
    rows = 16
    inverse = 1.0 / (jnp.sqrt(total) + 1e-07)
    update_scale = 0.2 * math.sqrt(max(size, width))

    @pl.loop(0, size // rows)
    def _(i):
        part = pl.ds(pl.multiple_of(i * rows, rows), rows)
        x[part, :] = (x[part, :].astype(jnp.float32) * inverse).astype(jnp.bfloat16)

    @pl.loop(0, NS_STEPS)
    def _(iteration):
        gram[...] = dot_nt(x[...], x[...]).astype(jnp.bfloat16)
        g = gram[...]
        poly[...] = (coeff_b * g.astype(jnp.float32) + coeff_c * dot_nn(g, g)).astype(jnp.bfloat16)
        v = x[...]
        x[...] = (coeff_a * v.astype(jnp.float32) + dot_nn(poly[...], v)).astype(jnp.bfloat16)

    @pl.loop(0, size // rows)
    def _(i):
        part = pl.ds(pl.multiple_of(i * rows, rows), rows)
        x[part, :] = (update_scale * x[part, :].astype(jnp.float32)).astype(jnp.bfloat16)


def step_kernel(
    shards, keep, y, gn, go, w, nt_a, nt_b, nw, update,
    yv, yb, yp, ub, up, gnv, gov, gs, wv, wp, w1v, w1p, nwv, urv, xv, gram, poly,
    y_sem, yb_send, yb_recv, u_send, u_recv, g_send, g_recv, nt_sem, r_send, r_recv, nw_sem, up_sem,
    in_sem, w_send, w_recv, v_send, v_recv, heard_x, heard_y,
):
    rep, me = lax.axis_index("rep"), lax.axis_index("shard")
    core = rep + 1 - 2 * lax.rem(rep, 2)
    side = lax.rem(rep + 2, 4)
    rows = gs.shape[1]
    pieces = v_send.shape[0]
    span = shards // pieces
    enter = greet(rep, me, (core, side))
    at = lambda step: peer_at(me, step, shards)
    block = lambda e: pl.ds(pl.multiple_of(e * rows, rows), rows)

    def load_y(step):
        return pltpu.make_async_copy(y.at[at(step)], yv.at[at(step)], y_sem.at[step])

    def send_y(step):
        e = at(step)
        return pltpu.make_async_remote_copy(
            yb.at[e], yp.at[e], yb_send.at[step], yb_recv.at[step], device_id=(core, me), device_id_type=MESH
        )

    def send_u(step):
        e = at(step)
        return pltpu.make_async_remote_copy(
            ub.at[e], up.at[e], u_send.at[step], u_recv.at[step], device_id=(side, me), device_id_type=MESH
        )

    def send_g(step):
        e = at(step)
        return pltpu.make_async_remote_copy(
            gs.at[e], xv.at[block(me)], g_send.at[step], g_recv.at[step], device_id=(rep, e), device_id_type=MESH
        )

    def send_w1(piece):
        part = pl.ds(piece * span, span)
        return pltpu.make_async_remote_copy(
            w1v.at[part], w1p.at[part], v_send.at[piece], v_recv.at[piece], device_id=(side, me), device_id_type=MESH
        )

    def send_back(step):
        e = at(step)
        return pltpu.make_async_remote_copy(
            xv.at[block(e)], urv.at[me], r_send.at[step], r_recv.at[step], device_id=(rep, e), device_id_type=MESH
        )

    def store_nt(step, half):
        e = at(step)
        width = nt_a.shape[2]
        return pltpu.make_async_copy(
            yv.at[e, :, pl.ds(half * width, width)], (nt_a, nt_b)[half].at[e], nt_sem.at[half, step]
        )

    def store_nw(step):
        return pltpu.make_async_copy(nwv.at[at(step)], nw.at[at(step)], nw_sem.at[step])

    def store_update(step):
        return pltpu.make_async_copy(urv.at[at(step)], update.at[at(step)], up_sem.at[step])

    load_gn = pltpu.make_async_copy(gn, gnv, in_sem.at[0])
    load_go = pltpu.make_async_copy(go, gov, in_sem.at[1])
    load_w = pltpu.make_async_copy(w, wv, in_sem.at[2])
    send_w = pltpu.make_async_remote_copy(wv, wp, w_send, w_recv, device_id=(core, me), device_id_type=MESH)

    @pl.loop(0, shards)
    def _(step):
        load_y(step).start()

    load_gn.start()
    load_go.start()
    load_w.start()
    own0, other0 = shares(keep, rep, 0)
    own1, other1 = shares(keep, rep, 1)

    def narrow(step):
        load_y(step).wait()
        e = at(step)
        yb[e] = yv[e].astype(jnp.bfloat16)

    pl.loop(0, HEAD)(narrow)
    enter()
    all_x = relay(rep, me, LINES[0], heard_x)

    @pl.loop(0, HEAD - 1)
    def _(step):
        send_y(step).start()

    @pl.loop(HEAD, shards + LAG + 1)
    def _(tick):
        @pl.when(tick < shards)
        def _():
            narrow(tick)

        @pl.when((tick >= 1) & (tick <= shards))
        def _():
            send_y(tick - 1).start()

        @pl.when((tick >= LAG) & (tick < shards + LAG))
        def _():
            send_y(tick - LAG).wait_recv()
            e = at(tick - LAG)
            mixed = own0 * yv[e] + other0 * yp[e].astype(jnp.float32)
            yv[e] = mixed
            ub[e] = mixed.astype(jnp.bfloat16)

        @pl.when(tick >= LAG + 1)
        def _():
            send_u(tick - LAG - 1).start()

    all_x()
    all_y = relay(rep, me, LINES[1], heard_y)
    load_w.wait()
    send_w.start()
    all_y()
    load_gn.wait()
    load_go.wait()

    @pl.loop(0, shards + 1)
    def _(tick):
        @pl.when(tick < shards)
        def _():
            send_u(tick).wait_recv()
            e = at(tick)
            fresh = (
                own1 * yv[e] + other1 * up[e].astype(jnp.float32)
                + gnv[e].astype(jnp.float32) - gov[e].astype(jnp.float32)
            )
            yv[e] = fresh
            gs[e] = fresh.astype(jnp.bfloat16)

        @pl.when(tick >= 2)
        def _():
            send_g(tick - 1).start()

        @pl.when(tick >= 1)
        def _():
            store_nt(tick - 1, 0).start()
            store_nt(tick - 1, 1).start()

    send_w.wait()

    @pl.loop(0, shards)
    def _(e):
        w1v[e] = (own0 * wv[e].astype(jnp.float32) + other0 * wp[e].astype(jnp.float32)).astype(jnp.bfloat16)

    xv[block(me), :] = gs[me]

    @pl.loop(0, pieces)
    def _(piece):
        send_w1(piece).start()

    def square(step, total):
        @pl.when(step >= 1)
        def _():
            send_g(step).wait_recv()

        part = xv[block(at(step)), :].astype(jnp.float32)
        return total + part * part

    total = lax.fori_loop(0, shards, square, jnp.zeros((rows, xv.shape[1]), jnp.float32))
    newton_schulz(xv, gram, poly, jnp.sum(total))

    @pl.loop(1, shards)
    def _(step):
        send_back(step).start()

    urv[me] = xv[block(me), :]

    @pl.loop(0, shards)
    def _(step):
        send_y(step).wait_send()
        send_u(step).wait_send()
        store_nt(step, 0).wait()
        store_nt(step, 1).wait()

    @pl.loop(1, shards)
    def _(step):
        send_g(step).wait_send()

    @pl.loop(0, pieces)
    def _(piece):
        send_w1(piece).wait()

    @pl.loop(0, shards)
    def _(e):
        nwv[e] = (own1 * w1v[e].astype(jnp.float32) + other1 * w1p[e].astype(jnp.float32)).astype(jnp.bfloat16)

    @pl.loop(0, shards + 1)
    def _(tick):
        @pl.when(tick < shards)
        def _():
            @pl.when(tick >= 1)
            def _():
                send_back(tick).wait_recv()

            e = at(tick)
            nwv[e] = (nwv[e].astype(jnp.float32) - learn_rate * urv[e].astype(jnp.float32)).astype(jnp.bfloat16)

        @pl.when(tick >= 1)
        def _():
            store_nw(tick - 1).start()
            store_update(tick - 1).start()

    @pl.loop(1, shards)
    def _(step):
        send_back(step).wait_send()

    @pl.loop(0, shards)
    def _(step):
        store_nw(step).wait()
        store_update(step).wait()


def eject_kernel(a, b, c, d, nt, nw, update, sem):
    width = a.shape[2]
    pairs = [(a, nt.at[:, :, pl.ds(0, width)]), (b, nt.at[:, :, pl.ds(width, width)]), (c, nw), (d, update)]
    copies = [pltpu.make_async_copy(x, o, sem.at[i]) for i, (x, o) in enumerate(pairs)]
    for copy in copies:
        copy.start()
    for copy in copies:
        copy.wait()


def local(weight, tracker, grad_new, grad_old, mix_keep):
    shards = lax.axis_size("shard")
    block = weight.shape[1:]
    experts, rows, columns = block
    size = shards * rows
    half = jax.ShapeDtypeStruct(block, jnp.bfloat16)
    full = jax.ShapeDtypeStruct(block, jnp.float32)
    part = jax.ShapeDtypeStruct((experts, rows, columns // 2), jnp.float32)
    anywhere = pl.BlockSpec(memory_space=pl.ANY)
    scalars = pl.BlockSpec(memory_space=pltpu.SMEM)
    dma = pltpu.SemaphoreType.DMA

    made = pl.pallas_call(
        functools.partial(step_kernel, shards),
        out_shape=(part, part, half, half),
        in_specs=[scalars] + [pl.BlockSpec(memory_space=pltpu.HBM)] * 4,
        out_specs=(anywhere,) * 4,
        scratch_shapes=[pltpu.VMEM(block, jnp.float32)] + [pltpu.VMEM(block, jnp.bfloat16)] * 13
        + [pltpu.VMEM((size, columns), jnp.bfloat16)] + [pltpu.VMEM((size, size), jnp.bfloat16)] * 2
        + [dma((shards,))] * 7 + [dma((2, shards))] + [dma((shards,))] * 4 + [dma((3,)), dma, dma, dma((4,)), dma((4,))] + [pltpu.SemaphoreType.REGULAR] * 2,
        compiler_params=pltpu.CompilerParams(collective_id=0, has_side_effects=True, vmem_limit_bytes=48 << 20),
        name="step",
    )(mix_keep.T, tracker[0], grad_new[0], grad_old[0], weight[0])
    new_tracker, new_weight, update = pl.pallas_call(
        eject_kernel,
        out_shape=(full, half, half),
        in_specs=[anywhere] * 4,
        out_specs=(pl.BlockSpec(memory_space=pltpu.HBM),) * 3,
        scratch_shapes=[dma((4,))],
        compiler_params=pltpu.CompilerParams(vmem_limit_bytes=1 << 20),
        name="eject",
    )(*made)
    return (new_weight[None], new_tracker[None], update[None])


def solution(mesh):
    spec = P("rep", None, "shard", None)
    return jax.shard_map(
        local,
        mesh=mesh,
        in_specs=(spec, spec, spec, spec, P()),
        out_specs=(spec, spec, spec),
        check_vma=False,
    )
```

```python
import functools
import math

import jax
import jax.numpy as jnp
from jax import lax
from jax.experimental import pallas as pl
from jax.experimental.pallas import tpu as pltpu
from jax.sharding import PartitionSpec as P

MESH = pl.DeviceIdType.MESH
NS_STEPS = 5

coeff_a = 3.4445
coeff_b = -4.775
coeff_c = 2.0315
learn_rate = 0.05

STRIDE = 13
HEAD = 8
LAG = 14
AHEAD = 4


def peer_at(me, step, shards):
    return lax.bitwise_xor(me, lax.bitwise_and(step * STRIDE, shards - 1))


LINES = ((1, 2, 3), (8, 16, 24), (4,))


def greet(rep, me, others):
    barrier = pltpu.get_barrier_semaphore()
    near = [(rep, lax.bitwise_xor(me, bits)) for line in LINES for bits in line] + [(other, me) for other in others]
    for device in near:
        pl.semaphore_signal(barrier, inc=1, device_id=device, device_id_type=MESH)
    return lambda: pl.semaphore_wait(barrier, len(near))


def relay(rep, me, line, heard):
    for bits in line:
        pl.semaphore_signal(heard, inc=1, device_id=(rep, lax.bitwise_xor(me, bits)), device_id_type=MESH)
    return lambda: pl.semaphore_wait(heard, len(line))


def shares(keep, rep, bit):
    own = keep[bit, rep].astype(jnp.float32) / 16.0
    return own, 1.0 - own


def dot_nt(a, b):
    return lax.dot_general(a, b, (((1,), (1,)), ((), ())), preferred_element_type=jnp.float32)


def dot_nn(a, b):
    return lax.dot_general(a, b, (((1,), (0,)), ((), ())), preferred_element_type=jnp.float32)


def newton_schulz(x, gram, poly, total):
    size, width = x.shape
    rows = 16
    inverse = 1.0 / (jnp.sqrt(total) + 1e-07)
    update_scale = 0.2 * math.sqrt(max(size, width))

    @pl.loop(0, size // rows)
    def _(i):
        part = pl.ds(pl.multiple_of(i * rows, rows), rows)
        x[part, :] = (x[part, :].astype(jnp.float32) * inverse).astype(jnp.bfloat16)

    @pl.loop(0, NS_STEPS)
    def _(iteration):
        gram[...] = dot_nt(x[...], x[...]).astype(jnp.bfloat16)
        g = gram[...]
        poly[...] = (coeff_b * g.astype(jnp.float32) + coeff_c * dot_nn(g, g)).astype(jnp.bfloat16)
        v = x[...]
        x[...] = (coeff_a * v.astype(jnp.float32) + dot_nn(poly[...], v)).astype(jnp.bfloat16)

    @pl.loop(0, size // rows)
    def _(i):
        part = pl.ds(pl.multiple_of(i * rows, rows), rows)
        x[part, :] = (update_scale * x[part, :].astype(jnp.float32)).astype(jnp.bfloat16)


def step_kernel(
    shards, keep, y, gn, go, w, nt, nw, update,
    yb, yp, ub, up, gnv, gov, gs, wv, wp, w1v, w1p, wz, wzp, xv, gram, poly,
    y_sem, yb_send, yb_recv, u_send, u_recv, g_send, g_recv, r_send, r_recv,
    in_sem, w_send, w_recv, v_send, v_recv, heard_x, heard_y, ahead_sem,
):
    rep, me = lax.axis_index("rep"), lax.axis_index("shard")
    core = rep + 1 - 2 * lax.rem(rep, 2)
    side = lax.rem(rep + 2, 4)
    rows = gs.shape[1]
    pieces = v_send.shape[0]
    ahead = wz.shape[0]
    span = (shards - ahead) // pieces
    enter = greet(rep, me, (core, side))
    at = lambda step: peer_at(me, step, shards)
    block = lambda e: pl.ds(pl.multiple_of(e * rows, rows), rows)

    def load_y(step):
        return pltpu.make_async_copy(y.at[at(step)], nt.at[at(step)], y_sem.at[step])

    def send_y(step):
        e = at(step)
        return pltpu.make_async_remote_copy(
            yb.at[e], yp.at[e], yb_send.at[step], yb_recv.at[step], device_id=(core, me), device_id_type=MESH
        )

    def send_u(step):
        e = at(step)
        return pltpu.make_async_remote_copy(
            ub.at[e], up.at[e], u_send.at[step], u_recv.at[step], device_id=(side, me), device_id_type=MESH
        )

    def send_g(step):
        e = at(step)
        return pltpu.make_async_remote_copy(
            gs.at[e], xv.at[block(me)], g_send.at[step], g_recv.at[step], device_id=(rep, e), device_id_type=MESH
        )

    def send_w1(piece):
        part = pl.ds(ahead + piece * span, span)
        return pltpu.make_async_remote_copy(
            w1v.at[part], w1p.at[part], v_send.at[piece], v_recv.at[piece], device_id=(side, me), device_id_type=MESH
        )

    def send_back(step):
        e = at(step)
        return pltpu.make_async_remote_copy(
            xv.at[block(e)], update.at[me], r_send.at[step], r_recv.at[step], device_id=(rep, e), device_id_type=MESH
        )

    load_gn = pltpu.make_async_copy(gn, gnv, in_sem.at[0])
    load_go = pltpu.make_async_copy(go, gov, in_sem.at[1])
    load_w = pltpu.make_async_copy(w, wv, in_sem.at[2])
    send_w = pltpu.make_async_remote_copy(wv, wp, w_send, w_recv, device_id=(core, me), device_id_type=MESH)

    early = pltpu.make_async_remote_copy(
        w.at[pl.ds(0, ahead)], wz, ahead_sem.at[0], ahead_sem.at[1], device_id=(side, me), device_id_type=MESH
    )
    early_across = pltpu.make_async_remote_copy(
        wz, wzp, ahead_sem.at[2], ahead_sem.at[3], device_id=(core, me), device_id_type=MESH
    )

    @pl.loop(0, shards)
    def _(step):
        load_y(step).start()

    load_gn.start()
    load_go.start()
    load_w.start()
    own0, other0 = shares(keep, rep, 0)
    own1, other1 = shares(keep, rep, 1)

    def narrow(step):
        load_y(step).wait()
        e = at(step)
        yb[e] = nt[e].astype(jnp.bfloat16)

    pl.loop(0, HEAD)(narrow)
    enter()
    early.start()
    all_x = relay(rep, me, LINES[0], heard_x)

    @pl.loop(0, HEAD - 1)
    def _(step):
        send_y(step).start()

    @pl.loop(HEAD, shards + LAG + 1)
    def _(tick):
        @pl.when(tick < shards)
        def _():
            narrow(tick)

        @pl.when((tick >= 1) & (tick <= shards))
        def _():
            send_y(tick - 1).start()

        @pl.when((tick >= LAG) & (tick < shards + LAG))
        def _():
            send_y(tick - LAG).wait_recv()
            e = at(tick - LAG)
            mixed = own0 * nt[e] + other0 * yp[e].astype(jnp.float32)
            nt[e] = mixed
            ub[e] = mixed.astype(jnp.bfloat16)

        @pl.when(tick >= LAG + 1)
        def _():
            send_u(tick - LAG - 1).start()

    all_x()
    all_y = relay(rep, me, LINES[1], heard_y)
    load_w.wait()
    send_w.start()
    all_y()
    load_gn.wait()
    load_go.wait()

    @pl.loop(0, shards + 1)
    def _(tick):
        @pl.when(tick < shards)
        def _():
            send_u(tick).wait_recv()
            e = at(tick)
            fresh = (
                own1 * nt[e] + other1 * up[e].astype(jnp.float32)
                + gnv[e].astype(jnp.float32) - gov[e].astype(jnp.float32)
            )
            nt[e] = fresh
            gs[e] = fresh.astype(jnp.bfloat16)

        @pl.when(tick >= 2)
        def _():
            send_g(tick - 1).start()

    send_w.wait()
    early.wait()
    early_across.start()

    @pl.loop(0, shards)
    def _(e):
        w1v[e] = (own0 * wv[e].astype(jnp.float32) + other0 * wp[e].astype(jnp.float32)).astype(jnp.bfloat16)

    xv[block(me), :] = gs[me]

    @pl.loop(0, pieces)
    def _(piece):
        send_w1(piece).start()

    def square(step, total):
        @pl.when(step >= 1)
        def _():
            send_g(step).wait_recv()

        part = xv[block(at(step)), :].astype(jnp.float32)
        return total + part * part

    total = lax.fori_loop(0, shards, square, jnp.zeros((rows, xv.shape[1]), jnp.float32))
    newton_schulz(xv, gram, poly, jnp.sum(total))

    @pl.loop(1, shards)
    def _(step):
        send_back(step).start()

    update[me] = xv[block(me), :]

    @pl.loop(0, shards)
    def _(step):
        send_y(step).wait_send()
        send_u(step).wait_send()

    @pl.loop(1, shards)
    def _(step):
        send_g(step).wait_send()

    early_across.wait()
    side_own0, side_other0 = shares(keep, side, 0)

    @pl.loop(0, ahead)
    def _(e):
        w1p[e] = (side_own0 * wz[e].astype(jnp.float32) + side_other0 * wzp[e].astype(jnp.float32)).astype(jnp.bfloat16)

    @pl.loop(0, pieces)
    def _(piece):
        send_w1(piece).wait()

    @pl.loop(0, shards)
    def _(e):
        nw[e] = (own1 * w1v[e].astype(jnp.float32) + other1 * w1p[e].astype(jnp.float32)).astype(jnp.bfloat16)

    @pl.loop(0, shards)
    def _(step):
        @pl.when(step >= 1)
        def _():
            send_back(step).wait_recv()

        e = at(step)
        nw[e] = (nw[e].astype(jnp.float32) - learn_rate * update[e].astype(jnp.float32)).astype(jnp.bfloat16)

    @pl.loop(1, shards)
    def _(step):
        send_back(step).wait_send()


def eject_kernel(a, b, c, nt, nw, update, sem):
    copies = [pltpu.make_async_copy(x, o, sem.at[i]) for i, (x, o) in enumerate([(a, nt), (b, nw), (c, update)])]
    for copy in copies:
        copy.start()
    for copy in copies:
        copy.wait()


def local(weight, tracker, grad_new, grad_old, mix_keep):
    shards = lax.axis_size("shard")
    block = weight.shape[1:]
    experts, rows, columns = block
    size = shards * rows
    half = jax.ShapeDtypeStruct(block, jnp.bfloat16)
    full = jax.ShapeDtypeStruct(block, jnp.float32)
    anywhere = pl.BlockSpec(memory_space=pl.ANY)
    scalars = pl.BlockSpec(memory_space=pltpu.SMEM)
    dma = pltpu.SemaphoreType.DMA

    made = pl.pallas_call(
        functools.partial(step_kernel, shards),
        out_shape=(pltpu.VMEM(block, jnp.float32), pltpu.VMEM(block, jnp.bfloat16), pltpu.VMEM(block, jnp.bfloat16)),
        in_specs=[scalars] + [pl.BlockSpec(memory_space=pltpu.HBM)] * 4,
        out_specs=(pl.BlockSpec(memory_space=pltpu.VMEM),) * 3,
        scratch_shapes=[pltpu.VMEM(block, jnp.bfloat16)] * 11
        + [pltpu.VMEM((AHEAD, rows, columns), jnp.bfloat16)] * 2
        + [pltpu.VMEM((size, columns), jnp.bfloat16)] + [pltpu.VMEM((size, size), jnp.bfloat16)] * 2
        + [dma((shards,))] * 9 + [dma((3,)), dma, dma, dma((4,)), dma((4,))] + [pltpu.SemaphoreType.REGULAR] * 2 + [dma((4,))],
        compiler_params=pltpu.CompilerParams(collective_id=0, has_side_effects=True, vmem_limit_bytes=48 << 20),
        name="step",
    )(mix_keep.T, tracker[0], grad_new[0], grad_old[0], weight[0])
    new_tracker, new_weight, update = pl.pallas_call(
        eject_kernel,
        out_shape=(full, half, half),
        in_specs=[pl.BlockSpec(memory_space=pltpu.VMEM)] * 3,
        out_specs=(pl.BlockSpec(memory_space=pltpu.HBM),) * 3,
        scratch_shapes=[dma((3,))],
        compiler_params=pltpu.CompilerParams(vmem_limit_bytes=1 << 20),
        name="eject",
    )(*made)
    return (new_weight[None], new_tracker[None], update[None])


def solution(mesh):
    spec = P("rep", None, "shard", None)
    return jax.shard_map(
        local,
        mesh=mesh,
        in_specs=(spec, spec, spec, spec, P()),
        out_specs=(spec, spec, spec),
        check_vma=False,
    )
```

```python
import functools
import math

import jax
import jax.numpy as jnp
from jax import lax
from jax.experimental import pallas as pl
from jax.experimental.pallas import tpu as pltpu
from jax.sharding import PartitionSpec as P

MESH = pl.DeviceIdType.MESH
NS_STEPS = 5

coeff_a = 3.4445
coeff_b = -4.775
coeff_c = 2.0315
learn_rate = 0.05

STRIDE = 13
HEAD = 8
LAG = 14
AHEAD = 4
LATE = 8


def peer_at(me, step, shards):
    return lax.bitwise_xor(me, lax.bitwise_and(step * STRIDE, shards - 1))


LINES = ((1, 2, 3), (8, 16, 24), (4,))


def greet(rep, me, others):
    barrier = pltpu.get_barrier_semaphore()
    near = [(rep, lax.bitwise_xor(me, bits)) for line in LINES for bits in line] + [(other, me) for other in others]
    for device in near:
        pl.semaphore_signal(barrier, inc=1, device_id=device, device_id_type=MESH)
    return lambda: pl.semaphore_wait(barrier, len(near))


def relay(rep, me, line, heard):
    for bits in line:
        pl.semaphore_signal(heard, inc=1, device_id=(rep, lax.bitwise_xor(me, bits)), device_id_type=MESH)
    return lambda: pl.semaphore_wait(heard, len(line))


def shares(keep, rep, bit):
    own = keep[bit, rep].astype(jnp.float32) / 16.0
    return own, 1.0 - own


def dot_nt(a, b):
    return lax.dot_general(a, b, (((1,), (1,)), ((), ())), preferred_element_type=jnp.float32)


def dot_nn(a, b):
    return lax.dot_general(a, b, (((1,), (0,)), ((), ())), preferred_element_type=jnp.float32)


def newton_schulz(x, gram, poly, total):
    size, width = x.shape
    rows = 16
    inverse = 1.0 / (jnp.sqrt(total) + 1e-07)
    update_scale = 0.2 * math.sqrt(max(size, width))

    @pl.loop(0, size // rows)
    def _(i):
        part = pl.ds(pl.multiple_of(i * rows, rows), rows)
        x[part, :] = (x[part, :].astype(jnp.float32) * inverse).astype(jnp.bfloat16)

    @pl.loop(0, NS_STEPS)
    def _(iteration):
        gram[...] = dot_nt(x[...], x[...]).astype(jnp.bfloat16)
        g = gram[...]
        poly[...] = (coeff_b * g.astype(jnp.float32) + coeff_c * dot_nn(g, g)).astype(jnp.bfloat16)
        v = x[...]
        x[...] = (coeff_a * v.astype(jnp.float32) + dot_nn(poly[...], v)).astype(jnp.bfloat16)

    @pl.loop(0, size // rows)
    def _(i):
        part = pl.ds(pl.multiple_of(i * rows, rows), rows)
        x[part, :] = (update_scale * x[part, :].astype(jnp.float32)).astype(jnp.bfloat16)


def step_kernel(
    shards, keep, y, gn, go, w, nt, nw, update,
    yb, yp, ub, up, gnv, gov, gs, wv, wp, w1v, w1p, wz, wzp, xv, gram, poly,
    y_sem, yb_send, yb_recv, u_send, u_recv, g_send, g_recv, r_send, r_recv,
    in_sem, w_send, w_recv, v_send, v_recv, heard_x, heard_y, ahead_sem, l_send, l_recv,
):
    rep, me = lax.axis_index("rep"), lax.axis_index("shard")
    core = rep + 1 - 2 * lax.rem(rep, 2)
    side = lax.rem(rep + 2, 4)
    rows = gs.shape[1]
    pieces = v_send.shape[0]
    ahead = wz.shape[0]
    late = l_send.shape[0]
    first_late = shards - late
    span = (first_late - ahead) // pieces
    enter = greet(rep, me, (core, side))
    at = lambda step: peer_at(me, step, shards)
    block = lambda e: pl.ds(pl.multiple_of(e * rows, rows), rows)

    def load_y(step):
        return pltpu.make_async_copy(y.at[at(step)], nt.at[at(step)], y_sem.at[step])

    def send_y(step):
        e = at(step)
        return pltpu.make_async_remote_copy(
            yb.at[e], yp.at[e], yb_send.at[step], yb_recv.at[step], device_id=(core, me), device_id_type=MESH
        )

    def send_u(step):
        e = at(step)
        return pltpu.make_async_remote_copy(
            ub.at[e], up.at[e], u_send.at[step], u_recv.at[step], device_id=(side, me), device_id_type=MESH
        )

    def send_g(step):
        e = at(step)
        return pltpu.make_async_remote_copy(
            gs.at[e], xv.at[block(me)], g_send.at[step], g_recv.at[step], device_id=(rep, e), device_id_type=MESH
        )

    def send_w1(piece):
        part = pl.ds(ahead + piece * span, span)
        return pltpu.make_async_remote_copy(
            w1v.at[part], w1p.at[part], v_send.at[piece], v_recv.at[piece], device_id=(side, me), device_id_type=MESH
        )

    def send_late(i):
        e = first_late + i
        return pltpu.make_async_remote_copy(
            w1v.at[e], w1p.at[e], l_send.at[i], l_recv.at[i], device_id=(side, me), device_id_type=MESH
        )

    def send_back(step):
        e = at(step)
        return pltpu.make_async_remote_copy(
            xv.at[block(e)], update.at[me], r_send.at[step], r_recv.at[step], device_id=(rep, e), device_id_type=MESH
        )

    load_gn = pltpu.make_async_copy(gn, gnv, in_sem.at[0])
    load_go = pltpu.make_async_copy(go, gov, in_sem.at[1])
    load_w = pltpu.make_async_copy(w, wv, in_sem.at[2])
    send_w = pltpu.make_async_remote_copy(wv, wp, w_send, w_recv, device_id=(core, me), device_id_type=MESH)

    early = pltpu.make_async_remote_copy(
        w.at[pl.ds(0, ahead)], wz, ahead_sem.at[0], ahead_sem.at[1], device_id=(side, me), device_id_type=MESH
    )
    early_across = pltpu.make_async_remote_copy(
        wz, wzp, ahead_sem.at[2], ahead_sem.at[3], device_id=(core, me), device_id_type=MESH
    )

    @pl.loop(0, shards)
    def _(step):
        load_y(step).start()

    load_gn.start()
    load_go.start()
    load_w.start()
    own0, other0 = shares(keep, rep, 0)
    own1, other1 = shares(keep, rep, 1)

    def narrow(step):
        load_y(step).wait()
        e = at(step)
        yb[e] = nt[e].astype(jnp.bfloat16)

    enter()
    early.start()
    pl.loop(0, HEAD)(narrow)
    all_x = relay(rep, me, LINES[0], heard_x)

    @pl.loop(0, HEAD - 1)
    def _(step):
        send_y(step).start()

    @pl.loop(HEAD, shards + LAG + 1)
    def _(tick):
        @pl.when(tick < shards)
        def _():
            narrow(tick)

        @pl.when((tick >= 1) & (tick <= shards))
        def _():
            send_y(tick - 1).start()

        @pl.when((tick >= LAG) & (tick < shards + LAG))
        def _():
            send_y(tick - LAG).wait_recv()
            e = at(tick - LAG)
            mixed = own0 * nt[e] + other0 * yp[e].astype(jnp.float32)
            nt[e] = mixed
            ub[e] = mixed.astype(jnp.bfloat16)

        @pl.when(tick >= LAG + 1)
        def _():
            send_u(tick - LAG - 1).start()

    all_x()
    all_y = relay(rep, me, LINES[1], heard_y)
    load_w.wait()
    send_w.start()
    all_y()
    load_gn.wait()
    load_go.wait()

    @pl.loop(0, shards + 1)
    def _(tick):
        @pl.when(tick < shards)
        def _():
            send_u(tick).wait_recv()
            e = at(tick)
            fresh = (
                own1 * nt[e] + other1 * up[e].astype(jnp.float32)
                + gnv[e].astype(jnp.float32) - gov[e].astype(jnp.float32)
            )
            nt[e] = fresh
            gs[e] = fresh.astype(jnp.bfloat16)

        @pl.when(tick >= 2)
        def _():
            send_g(tick - 1).start()

    send_w.wait()
    early.wait()
    early_across.start()

    @pl.loop(0, shards)
    def _(e):
        w1v[e] = (own0 * wv[e].astype(jnp.float32) + other0 * wp[e].astype(jnp.float32)).astype(jnp.bfloat16)

    xv[block(me), :] = gs[me]

    @pl.loop(0, pieces)
    def _(piece):
        send_w1(piece).start()

    def square(step, total):
        @pl.when(step >= 1)
        def _():
            send_g(step).wait_recv()

        part = xv[block(at(step)), :].astype(jnp.float32)
        return total + part * part

    total = lax.fori_loop(0, shards, square, jnp.zeros((rows, xv.shape[1]), jnp.float32))
    newton_schulz(xv, gram, poly, jnp.sum(total))

    @pl.loop(1, shards)
    def _(step):
        send_back(step).start()

    @pl.loop(0, late)
    def _(i):
        send_late(i).start()

    update[me] = xv[block(me), :]

    @pl.loop(0, shards)
    def _(step):
        send_y(step).wait_send()
        send_u(step).wait_send()

    @pl.loop(1, shards)
    def _(step):
        send_g(step).wait_send()

    early_across.wait()
    side_own0, side_other0 = shares(keep, side, 0)

    @pl.loop(0, ahead)
    def _(e):
        w1p[e] = (side_own0 * wz[e].astype(jnp.float32) + side_other0 * wzp[e].astype(jnp.float32)).astype(jnp.bfloat16)

    @pl.loop(0, pieces)
    def _(piece):
        send_w1(piece).wait()

    def mixed_weight(e):
        return (own1 * w1v[e].astype(jnp.float32) + other1 * w1p[e].astype(jnp.float32)).astype(jnp.bfloat16)

    def stepped(mixed, e):
        return (mixed.astype(jnp.float32) - learn_rate * update[e].astype(jnp.float32)).astype(jnp.bfloat16)

    @pl.loop(0, first_late)
    def _(e):
        nw[e] = mixed_weight(e)

    @pl.loop(0, shards)
    def _(step):
        @pl.when(step >= 1)
        def _():
            send_back(step).wait_recv()

        e = at(step)

        @pl.when(e < first_late)
        def _():
            nw[e] = stepped(nw[e], e)

    @pl.loop(0, late)
    def _(i):
        send_late(i).wait()
        e = first_late + i
        nw[e] = stepped(mixed_weight(e), e)

    @pl.loop(1, shards)
    def _(step):
        send_back(step).wait_send()


def eject_kernel(a, b, c, nt, nw, update, sem):
    copies = [pltpu.make_async_copy(x, o, sem.at[i]) for i, (x, o) in enumerate([(a, nt), (b, nw), (c, update)])]
    for copy in copies:
        copy.start()
    for copy in copies:
        copy.wait()


def local(weight, tracker, grad_new, grad_old, mix_keep):
    shards = lax.axis_size("shard")
    block = weight.shape[1:]
    experts, rows, columns = block
    size = shards * rows
    half = jax.ShapeDtypeStruct(block, jnp.bfloat16)
    full = jax.ShapeDtypeStruct(block, jnp.float32)
    anywhere = pl.BlockSpec(memory_space=pl.ANY)
    scalars = pl.BlockSpec(memory_space=pltpu.SMEM)
    dma = pltpu.SemaphoreType.DMA

    made = pl.pallas_call(
        functools.partial(step_kernel, shards),
        out_shape=(pltpu.VMEM(block, jnp.float32), pltpu.VMEM(block, jnp.bfloat16), pltpu.VMEM(block, jnp.bfloat16)),
        in_specs=[scalars] + [pl.BlockSpec(memory_space=pltpu.HBM)] * 4,
        out_specs=(pl.BlockSpec(memory_space=pltpu.VMEM),) * 3,
        scratch_shapes=[pltpu.VMEM(block, jnp.bfloat16)] * 11
        + [pltpu.VMEM((AHEAD, rows, columns), jnp.bfloat16)] * 2
        + [pltpu.VMEM((size, columns), jnp.bfloat16)] + [pltpu.VMEM((size, size), jnp.bfloat16)] * 2
        + [dma((shards,))] * 9 + [dma((3,)), dma, dma, dma((4,)), dma((4,))] + [pltpu.SemaphoreType.REGULAR] * 2 + [dma((4,))] + [dma((LATE,))] * 2,
        compiler_params=pltpu.CompilerParams(collective_id=0, has_side_effects=True, vmem_limit_bytes=48 << 20),
        name="step",
    )(mix_keep.T, tracker[0], grad_new[0], grad_old[0], weight[0])
    new_tracker, new_weight, update = pl.pallas_call(
        eject_kernel,
        out_shape=(full, half, half),
        in_specs=[pl.BlockSpec(memory_space=pltpu.VMEM)] * 3,
        out_specs=(pl.BlockSpec(memory_space=pltpu.HBM),) * 3,
        scratch_shapes=[dma((3,))],
        compiler_params=pltpu.CompilerParams(vmem_limit_bytes=1 << 20),
        name="eject",
    )(*made)
    return (new_weight[None], new_tracker[None], update[None])


def solution(mesh):
    spec = P("rep", None, "shard", None)
    return jax.shard_map(
        local,
        mesh=mesh,
        in_specs=(spec, spec, spec, spec, P()),
        out_specs=(spec, spec, spec),
        check_vma=False,
    )
```

```python
import functools
import math

import jax
import jax.numpy as jnp
from jax import lax
from jax.experimental import pallas as pl
from jax.experimental.pallas import tpu as pltpu
from jax.sharding import PartitionSpec as P

MESH = pl.DeviceIdType.MESH
NS_STEPS = 5

coeff_a = 3.4445
coeff_b = -4.775
coeff_c = 2.0315
learn_rate = 0.05

STRIDE = 13
HEAD = 8
LAG = 14
AHEAD = 4
LATE = 8
GROUP = 4
SENDS = 8


def peer_at(me, step, shards):
    return lax.bitwise_xor(me, lax.bitwise_and(step * STRIDE, shards - 1))


LINES = ((1, 2, 3), (8, 16, 24), (4,))


def greet(rep, me, others):
    barrier = pltpu.get_barrier_semaphore()
    near = [(rep, lax.bitwise_xor(me, bits)) for line in LINES for bits in line] + [(other, me) for other in others]
    for device in near:
        pl.semaphore_signal(barrier, inc=1, device_id=device, device_id_type=MESH)
    return lambda: pl.semaphore_wait(barrier, len(near))


def relay(rep, me, line, heard):
    for bits in line:
        pl.semaphore_signal(heard, inc=1, device_id=(rep, lax.bitwise_xor(me, bits)), device_id_type=MESH)
    return lambda: pl.semaphore_wait(heard, len(line))


def shares(keep, rep, bit):
    own = keep[bit, rep].astype(jnp.float32) / 16.0
    return own, 1.0 - own


def dot_nt(a, b):
    return lax.dot_general(a, b, (((1,), (1,)), ((), ())), preferred_element_type=jnp.float32)


def dot_nn(a, b):
    return lax.dot_general(a, b, (((1,), (0,)), ((), ())), preferred_element_type=jnp.float32)


def newton_schulz(x, gram, poly, total):
    size, width = x.shape
    rows = 16
    inverse = 1.0 / (jnp.sqrt(total) + 1e-07)
    update_scale = 0.2 * math.sqrt(max(size, width))

    @pl.loop(0, size // rows)
    def _(i):
        part = pl.ds(pl.multiple_of(i * rows, rows), rows)
        x[part, :] = (x[part, :].astype(jnp.float32) * inverse).astype(jnp.bfloat16)

    @pl.loop(0, NS_STEPS)
    def _(iteration):
        gram[...] = dot_nt(x[...], x[...]).astype(jnp.bfloat16)
        g = gram[...]
        poly[...] = (coeff_b * g.astype(jnp.float32) + coeff_c * dot_nn(g, g)).astype(jnp.bfloat16)
        v = x[...]
        x[...] = (coeff_a * v.astype(jnp.float32) + dot_nn(poly[...], v)).astype(jnp.bfloat16)

    @pl.loop(0, size // rows)
    def _(i):
        part = pl.ds(pl.multiple_of(i * rows, rows), rows)
        x[part, :] = (update_scale * x[part, :].astype(jnp.float32)).astype(jnp.bfloat16)


def step_kernel(
    shards, keep, y, gn, go, w, nt, nw, update,
    yb, yp, ub, up, gnv, gov, gs, wv, wp, w1v, w1p, wz, wzp, xv, gram, poly,
    y_sem, yb_send, yb_recv, u_send, u_recv, g_send, g_recv, r_send, r_recv,
    in_sem, w_send, w_recv, v_send, v_recv, heard_x, heard_y, ahead_sem, l_send, l_recv,
):
    rep, me = lax.axis_index("rep"), lax.axis_index("shard")
    core = rep + 1 - 2 * lax.rem(rep, 2)
    side = lax.rem(rep + 2, 4)
    rows = gs.shape[1]
    pieces = v_send.shape[0]
    ahead = wz.shape[0]
    late = l_send.shape[0]
    first_late = shards - late
    span = (first_late - ahead) // pieces
    enter = greet(rep, me, (core, side))
    at = lambda step: peer_at(me, step, shards)
    block = lambda e: pl.ds(pl.multiple_of(e * rows, rows), rows)

    def load_y(step):
        return pltpu.make_async_copy(y.at[at(step)], nt.at[at(step)], y_sem.at[lax.div(step, GROUP)])

    def send_y(step):
        e = at(step)
        return pltpu.make_async_remote_copy(
            yb.at[e], yp.at[e], yb_send.at[lax.div(step, SENDS)], yb_recv.at[lax.div(step, GROUP)], device_id=(core, me), device_id_type=MESH
        )

    def send_u(step):
        e = at(step)
        return pltpu.make_async_remote_copy(
            ub.at[e], up.at[e], u_send.at[lax.div(step, SENDS)], u_recv.at[lax.div(step, GROUP)], device_id=(side, me), device_id_type=MESH
        )

    def send_g(step):
        e = at(step)
        return pltpu.make_async_remote_copy(
            gs.at[e], xv.at[block(me)], g_send.at[lax.div(step, SENDS)], g_recv.at[lax.div(step, GROUP)], device_id=(rep, e), device_id_type=MESH
        )

    def send_w1(piece):
        part = pl.ds(ahead + piece * span, span)
        return pltpu.make_async_remote_copy(
            w1v.at[part], w1p.at[part], v_send.at[piece], v_recv.at[piece], device_id=(side, me), device_id_type=MESH
        )

    def send_late(i):
        e = first_late + i
        return pltpu.make_async_remote_copy(
            w1v.at[e], w1p.at[e], l_send.at[i], l_recv.at[i], device_id=(side, me), device_id_type=MESH
        )

    def send_back(step):
        e = at(step)
        return pltpu.make_async_remote_copy(
            xv.at[block(e)], update.at[me], r_send.at[step], r_recv.at[lax.div(step, GROUP)], device_id=(rep, e), device_id_type=MESH
        )

    def awaited(blocks, sent, received):
        return pltpu.make_async_remote_copy(
            blocks, blocks, sent, received, device_id=(core, me), device_id_type=MESH
        )

    def arrived(blocks, semaphore, step, missing):
        group = lax.div(step, GROUP)
        size = blocks.shape[0] // shards

        def wait(count):
            awaited(blocks.at[pl.ds(0, count * size)], y_sem.at[0], semaphore.at[group]).wait_recv()

        if missing:
            pl.when(step == 0)(lambda: wait(GROUP - missing))
            pl.when((step > 0) & (lax.rem(step, GROUP) == 0))(lambda: wait(GROUP))
        else:
            pl.when(lax.rem(step, GROUP) == 0)(lambda: wait(GROUP))

    def all_sent(blocks, semaphore, missing):
        size = blocks.shape[0] // shards
        if missing:
            awaited(blocks.at[pl.ds(0, (SENDS - missing) * size)], semaphore.at[0], y_sem.at[0]).wait_send()

        @pl.loop(1 if missing else 0, shards // SENDS)
        def _(group):
            awaited(blocks.at[pl.ds(0, SENDS * size)], semaphore.at[group], y_sem.at[0]).wait_send()

    load_gn = pltpu.make_async_copy(gn, gnv, in_sem.at[0])
    load_go = pltpu.make_async_copy(go, gov, in_sem.at[1])
    load_w = pltpu.make_async_copy(w, wv, in_sem.at[2])
    send_w = pltpu.make_async_remote_copy(wv, wp, w_send, w_recv, device_id=(core, me), device_id_type=MESH)

    early = pltpu.make_async_remote_copy(
        w.at[pl.ds(0, ahead)], wz, ahead_sem.at[0], ahead_sem.at[1], device_id=(side, me), device_id_type=MESH
    )
    early_across = pltpu.make_async_remote_copy(
        wz, wzp, ahead_sem.at[2], ahead_sem.at[3], device_id=(core, me), device_id_type=MESH
    )

    @pl.loop(0, shards)
    def _(step):
        load_y(step).start()

    load_gn.start()
    load_go.start()
    load_w.start()
    own0, other0 = shares(keep, rep, 0)
    own1, other1 = shares(keep, rep, 1)

    def narrow(step):
        @pl.when(lax.rem(step, GROUP) == 0)
        def _():
            part = pl.ds(0, GROUP)
            pltpu.make_async_copy(y.at[part], nt.at[part], y_sem.at[lax.div(step, GROUP)]).wait()

        e = at(step)
        yb[e] = nt[e].astype(jnp.bfloat16)

    enter()
    early.start()
    pl.loop(0, HEAD)(narrow)
    all_x = relay(rep, me, LINES[0], heard_x)

    @pl.loop(0, HEAD - 1)
    def _(step):
        send_y(step).start()

    @pl.loop(HEAD, shards + LAG + 1)
    def _(tick):
        @pl.when(tick < shards)
        def _():
            narrow(tick)

        @pl.when((tick >= 1) & (tick <= shards))
        def _():
            send_y(tick - 1).start()

        @pl.when((tick >= LAG) & (tick < shards + LAG))
        def _():
            arrived(yp, yb_recv, tick - LAG, 0)
            e = at(tick - LAG)
            mixed = own0 * nt[e] + other0 * yp[e].astype(jnp.float32)
            nt[e] = mixed
            ub[e] = mixed.astype(jnp.bfloat16)

        @pl.when(tick >= LAG + 1)
        def _():
            send_u(tick - LAG - 1).start()

    all_x()
    all_y = relay(rep, me, LINES[1], heard_y)
    load_w.wait()
    send_w.start()
    all_y()
    load_gn.wait()
    load_go.wait()

    @pl.loop(0, shards + 1)
    def _(tick):
        @pl.when(tick < shards)
        def _():
            arrived(up, u_recv, tick, 0)
            e = at(tick)
            fresh = (
                own1 * nt[e] + other1 * up[e].astype(jnp.float32)
                + gnv[e].astype(jnp.float32) - gov[e].astype(jnp.float32)
            )
            nt[e] = fresh
            gs[e] = fresh.astype(jnp.bfloat16)

        @pl.when(tick >= 2)
        def _():
            send_g(tick - 1).start()

    send_w.wait()
    early.wait()
    early_across.start()

    @pl.loop(0, shards)
    def _(e):
        w1v[e] = (own0 * wv[e].astype(jnp.float32) + other0 * wp[e].astype(jnp.float32)).astype(jnp.bfloat16)

    xv[block(me), :] = gs[me]

    @pl.loop(0, pieces)
    def _(piece):
        send_w1(piece).start()

    def square(step, total):
        arrived(xv, g_recv, step, 1)
        part = xv[block(at(step)), :].astype(jnp.float32)
        return total + part * part

    total = lax.fori_loop(0, shards, square, jnp.zeros((rows, xv.shape[1]), jnp.float32))
    newton_schulz(xv, gram, poly, jnp.sum(total))

    @pl.loop(1, shards)
    def _(step):
        send_back(step).start()

    @pl.loop(0, late)
    def _(i):
        send_late(i).start()

    update[me] = xv[block(me), :]

    all_sent(gs, g_send, 1)

    early_across.wait()
    side_own0, side_other0 = shares(keep, side, 0)

    @pl.loop(0, ahead)
    def _(e):
        w1p[e] = (side_own0 * wz[e].astype(jnp.float32) + side_other0 * wzp[e].astype(jnp.float32)).astype(jnp.bfloat16)

    all_sent(yb, yb_send, 0)

    all_sent(ub, u_send, 0)

    @pl.loop(0, pieces)
    def _(piece):
        send_w1(piece).wait()

    def mixed_weight(e):
        return (own1 * w1v[e].astype(jnp.float32) + other1 * w1p[e].astype(jnp.float32)).astype(jnp.bfloat16)

    def stepped(mixed, e):
        return (mixed.astype(jnp.float32) - learn_rate * update[e].astype(jnp.float32)).astype(jnp.bfloat16)

    @pl.loop(0, first_late)
    def _(e):
        nw[e] = mixed_weight(e)

    @pl.loop(0, shards)
    def _(step):
        arrived(update, r_recv, step, 1)
        e = at(step)

        @pl.when(e < first_late)
        def _():
            nw[e] = stepped(nw[e], e)

    @pl.loop(1, shards)
    def _(step):
        send_back(step).wait_send()

    @pl.loop(0, late)
    def _(i):
        send_late(i).wait()
        e = first_late + i
        nw[e] = stepped(mixed_weight(e), e)


def eject_kernel(a, b, c, nt, nw, update, sem):
    copies = [pltpu.make_async_copy(x, o, sem.at[i]) for i, (x, o) in enumerate([(a, nt), (b, nw), (c, update)])]
    for copy in copies:
        copy.start()
    for copy in copies:
        copy.wait()


def local(weight, tracker, grad_new, grad_old, mix_keep):
    shards = lax.axis_size("shard")
    block = weight.shape[1:]
    experts, rows, columns = block
    size = shards * rows
    half = jax.ShapeDtypeStruct(block, jnp.bfloat16)
    full = jax.ShapeDtypeStruct(block, jnp.float32)
    anywhere = pl.BlockSpec(memory_space=pl.ANY)
    scalars = pl.BlockSpec(memory_space=pltpu.SMEM)
    dma = pltpu.SemaphoreType.DMA

    made = pl.pallas_call(
        functools.partial(step_kernel, shards),
        out_shape=(pltpu.VMEM(block, jnp.float32), pltpu.VMEM(block, jnp.bfloat16), pltpu.VMEM(block, jnp.bfloat16)),
        in_specs=[scalars] + [pl.BlockSpec(memory_space=pltpu.HBM)] * 4,
        out_specs=(pl.BlockSpec(memory_space=pltpu.VMEM),) * 3,
        scratch_shapes=[pltpu.VMEM(block, jnp.bfloat16)] * 11
        + [pltpu.VMEM((AHEAD, rows, columns), jnp.bfloat16)] * 2
        + [pltpu.VMEM((size, columns), jnp.bfloat16)] + [pltpu.VMEM((size, size), jnp.bfloat16)] * 2
        + [dma((shards // GROUP,)), dma((shards // SENDS,)), dma((shards // GROUP,)), dma((shards // SENDS,)), dma((shards // GROUP,)), dma((shards // SENDS,)), dma((shards // GROUP,)), dma((shards,)), dma((shards // GROUP,))] + [dma((3,)), dma, dma, dma((4,)), dma((4,))] + [pltpu.SemaphoreType.REGULAR] * 2 + [dma((4,))] + [dma((LATE,))] * 2,
        compiler_params=pltpu.CompilerParams(collective_id=0, has_side_effects=True, vmem_limit_bytes=48 << 20),
        name="step",
    )(mix_keep.T, tracker[0], grad_new[0], grad_old[0], weight[0])
    new_tracker, new_weight, update = pl.pallas_call(
        eject_kernel,
        out_shape=(full, half, half),
        in_specs=[pl.BlockSpec(memory_space=pltpu.VMEM)] * 3,
        out_specs=(pl.BlockSpec(memory_space=pltpu.HBM),) * 3,
        scratch_shapes=[dma((3,))],
        compiler_params=pltpu.CompilerParams(vmem_limit_bytes=1 << 20),
        name="eject",
    )(*made)
    return (new_weight[None], new_tracker[None], update[None])


def solution(mesh):
    spec = P("rep", None, "shard", None)
    return jax.shard_map(
        local,
        mesh=mesh,
        in_specs=(spec, spec, spec, spec, P()),
        out_specs=(spec, spec, spec),
        check_vma=False,
    )
```

```python
import functools
import math

import jax
import jax.numpy as jnp
from jax import lax
from jax.experimental import pallas as pl
from jax.experimental.pallas import tpu as pltpu
from jax.sharding import PartitionSpec as P

MESH = pl.DeviceIdType.MESH
NS_STEPS = 5

coeff_a = 3.4445
coeff_b = -4.775
coeff_c = 2.0315
learn_rate = 0.05

STRIDE = 13
HEAD = 8
LAG = 14
AHEAD = 4
LATE = 8
GROUP = 8
SENDS = 8


def peer_at(me, step, shards):
    return lax.bitwise_xor(me, lax.bitwise_and(step * STRIDE, shards - 1))


LINES = ((1, 2, 3), (8, 16, 24), (4,))


def greet(rep, me, others):
    barrier = pltpu.get_barrier_semaphore()
    near = [(rep, lax.bitwise_xor(me, bits)) for line in LINES for bits in line] + [(other, me) for other in others]
    for device in near:
        pl.semaphore_signal(barrier, inc=1, device_id=device, device_id_type=MESH)
    return lambda: pl.semaphore_wait(barrier, len(near))


def relay(rep, me, line, heard):
    for bits in line:
        pl.semaphore_signal(heard, inc=1, device_id=(rep, lax.bitwise_xor(me, bits)), device_id_type=MESH)
    return lambda: pl.semaphore_wait(heard, len(line))


def shares(keep, rep, bit):
    own = keep[bit, rep].astype(jnp.float32) / 16.0
    return own, 1.0 - own


def dot_nt(a, b):
    return lax.dot_general(a, b, (((1,), (1,)), ((), ())), preferred_element_type=jnp.float32)


def dot_nn(a, b):
    return lax.dot_general(a, b, (((1,), (0,)), ((), ())), preferred_element_type=jnp.float32)


def newton_schulz(x, gram, poly, total):
    size, width = x.shape
    rows = 16
    inverse = 1.0 / (jnp.sqrt(total) + 1e-07)
    update_scale = 0.2 * math.sqrt(max(size, width))

    @pl.loop(0, size // rows)
    def _(i):
        part = pl.ds(pl.multiple_of(i * rows, rows), rows)
        x[part, :] = (x[part, :].astype(jnp.float32) * inverse).astype(jnp.bfloat16)

    @pl.loop(0, NS_STEPS)
    def _(iteration):
        gram[...] = dot_nt(x[...], x[...]).astype(jnp.bfloat16)
        g = gram[...]
        poly[...] = (coeff_b * g.astype(jnp.float32) + coeff_c * dot_nn(g, g)).astype(jnp.bfloat16)
        v = x[...]
        x[...] = (coeff_a * v.astype(jnp.float32) + dot_nn(poly[...], v)).astype(jnp.bfloat16)

    @pl.loop(0, size // rows)
    def _(i):
        part = pl.ds(pl.multiple_of(i * rows, rows), rows)
        x[part, :] = (update_scale * x[part, :].astype(jnp.float32)).astype(jnp.bfloat16)


def step_kernel(
    shards, keep, y, gn, go, w, nt, nw, update,
    yb, yp, ub, up, gnv, gov, gs, wv, wp, w1v, w1p, wz, wzp, xv, gram, poly,
    y_sem, yb_send, yb_recv, u_send, u_recv, g_send, g_recv, r_send, r_recv,
    in_sem, w_send, w_recv, v_send, v_recv, heard_x, heard_y, ahead_sem, l_send, l_recv,
):
    rep, me = lax.axis_index("rep"), lax.axis_index("shard")
    core = rep + 1 - 2 * lax.rem(rep, 2)
    side = lax.rem(rep + 2, 4)
    rows = gs.shape[1]
    pieces = v_send.shape[0]
    ahead = wz.shape[0]
    late = l_send.shape[0]
    first_late = shards - late
    span = (first_late - ahead) // pieces
    enter = greet(rep, me, (core, side))
    at = lambda step: peer_at(me, step, shards)
    block = lambda e: pl.ds(pl.multiple_of(e * rows, rows), rows)

    def load_y(step):
        return pltpu.make_async_copy(y.at[at(step)], nt.at[at(step)], y_sem.at[lax.div(step, GROUP)])

    def send_y(step):
        e = at(step)
        return pltpu.make_async_remote_copy(
            yb.at[e], yp.at[e], yb_send.at[lax.div(step, SENDS)], yb_recv.at[lax.div(step, GROUP)], device_id=(core, me), device_id_type=MESH
        )

    def send_u(step):
        e = at(step)
        return pltpu.make_async_remote_copy(
            ub.at[e], up.at[e], u_send.at[lax.div(step, SENDS)], u_recv.at[lax.div(step, GROUP)], device_id=(side, me), device_id_type=MESH
        )

    def send_g(step):
        e = at(step)
        return pltpu.make_async_remote_copy(
            gs.at[e], xv.at[block(me)], g_send.at[lax.div(step, SENDS)], g_recv.at[lax.div(step, GROUP)], device_id=(rep, e), device_id_type=MESH
        )

    def send_w1(piece):
        part = pl.ds(ahead + piece * span, span)
        return pltpu.make_async_remote_copy(
            w1v.at[part], w1p.at[part], v_send.at[piece], v_recv.at[piece], device_id=(side, me), device_id_type=MESH
        )

    def send_late(i):
        e = first_late + i
        return pltpu.make_async_remote_copy(
            w1v.at[e], w1p.at[e], l_send.at[i], l_recv.at[i], device_id=(side, me), device_id_type=MESH
        )

    def send_back(step):
        e = at(step)
        return pltpu.make_async_remote_copy(
            xv.at[block(e)], update.at[me], r_send.at[step], r_recv.at[lax.div(step, GROUP)], device_id=(rep, e), device_id_type=MESH
        )

    def awaited(blocks, sent, received):
        return pltpu.make_async_remote_copy(
            blocks, blocks, sent, received, device_id=(core, me), device_id_type=MESH
        )

    def arrived(blocks, semaphore, step, missing):
        group = lax.div(step, GROUP)
        size = blocks.shape[0] // shards

        def wait(count):
            awaited(blocks.at[pl.ds(0, count * size)], y_sem.at[0], semaphore.at[group]).wait_recv()

        if missing:
            pl.when(step == 0)(lambda: wait(GROUP - missing))
            pl.when((step > 0) & (lax.rem(step, GROUP) == 0))(lambda: wait(GROUP))
        else:
            pl.when(lax.rem(step, GROUP) == 0)(lambda: wait(GROUP))

    def all_sent(blocks, semaphore, missing):
        size = blocks.shape[0] // shards
        if missing:
            awaited(blocks.at[pl.ds(0, (SENDS - missing) * size)], semaphore.at[0], y_sem.at[0]).wait_send()

        @pl.loop(1 if missing else 0, shards // SENDS)
        def _(group):
            awaited(blocks.at[pl.ds(0, SENDS * size)], semaphore.at[group], y_sem.at[0]).wait_send()

    load_gn = pltpu.make_async_copy(gn, gnv, in_sem.at[0])
    load_go = pltpu.make_async_copy(go, gov, in_sem.at[1])
    load_w = pltpu.make_async_copy(w, wv, in_sem.at[2])
    send_w = pltpu.make_async_remote_copy(wv, wp, w_send, w_recv, device_id=(core, me), device_id_type=MESH)

    early = pltpu.make_async_remote_copy(
        w.at[pl.ds(0, ahead)], wz, ahead_sem.at[0], ahead_sem.at[1], device_id=(side, me), device_id_type=MESH
    )
    early_across = pltpu.make_async_remote_copy(
        wz, wzp, ahead_sem.at[2], ahead_sem.at[3], device_id=(core, me), device_id_type=MESH
    )

    @pl.loop(0, shards)
    def _(step):
        load_y(step).start()

    load_gn.start()
    load_go.start()
    load_w.start()
    own0, other0 = shares(keep, rep, 0)
    own1, other1 = shares(keep, rep, 1)

    def narrow(step):
        @pl.when(lax.rem(step, GROUP) == 0)
        def _():
            part = pl.ds(0, GROUP)
            pltpu.make_async_copy(y.at[part], nt.at[part], y_sem.at[lax.div(step, GROUP)]).wait()

        e = at(step)
        yb[e] = nt[e].astype(jnp.bfloat16)

    enter()
    early.start()
    pl.loop(0, HEAD)(narrow)
    all_x = relay(rep, me, LINES[0], heard_x)

    @pl.loop(0, HEAD - 1)
    def _(step):
        send_y(step).start()

    @pl.loop(HEAD, shards + LAG + 1)
    def _(tick):
        @pl.when(tick < shards)
        def _():
            narrow(tick)

        @pl.when((tick >= 1) & (tick <= shards))
        def _():
            send_y(tick - 1).start()

        @pl.when((tick >= LAG) & (tick < shards + LAG))
        def _():
            arrived(yp, yb_recv, tick - LAG, 0)
            e = at(tick - LAG)
            mixed = own0 * nt[e] + other0 * yp[e].astype(jnp.float32)
            nt[e] = mixed
            ub[e] = mixed.astype(jnp.bfloat16)

        @pl.when(tick >= LAG + 1)
        def _():
            send_u(tick - LAG - 1).start()

    all_x()
    all_y = relay(rep, me, LINES[1], heard_y)
    load_w.wait()
    send_w.start()
    all_y()
    load_gn.wait()
    load_go.wait()

    @pl.loop(0, shards + 1)
    def _(tick):
        @pl.when(tick < shards)
        def _():
            arrived(up, u_recv, tick, 0)
            e = at(tick)
            fresh = (
                own1 * nt[e] + other1 * up[e].astype(jnp.float32)
                + gnv[e].astype(jnp.float32) - gov[e].astype(jnp.float32)
            )
            nt[e] = fresh
            gs[e] = fresh.astype(jnp.bfloat16)

        @pl.when(tick >= 2)
        def _():
            send_g(tick - 1).start()

    send_w.wait()
    early.wait()
    early_across.start()

    @pl.loop(0, shards)
    def _(e):
        w1v[e] = (own0 * wv[e].astype(jnp.float32) + other0 * wp[e].astype(jnp.float32)).astype(jnp.bfloat16)

    xv[block(me), :] = gs[me]

    @pl.loop(0, pieces)
    def _(piece):
        send_w1(piece).start()

    def square(step, total):
        arrived(xv, g_recv, step, 1)
        part = xv[block(at(step)), :].astype(jnp.float32)
        return total + part * part

    total = lax.fori_loop(0, shards, square, jnp.zeros((rows, xv.shape[1]), jnp.float32))
    newton_schulz(xv, gram, poly, jnp.sum(total))

    @pl.loop(1, shards)
    def _(step):
        send_back(step).start()

    @pl.loop(0, late)
    def _(i):
        send_late(i).start()

    update[me] = xv[block(me), :]

    all_sent(gs, g_send, 1)

    early_across.wait()
    side_own0, side_other0 = shares(keep, side, 0)

    @pl.loop(0, ahead)
    def _(e):
        w1p[e] = (side_own0 * wz[e].astype(jnp.float32) + side_other0 * wzp[e].astype(jnp.float32)).astype(jnp.bfloat16)

    all_sent(yb, yb_send, 0)

    all_sent(ub, u_send, 0)

    @pl.loop(0, pieces)
    def _(piece):
        send_w1(piece).wait()

    def mixed_weight(e):
        return (own1 * w1v[e].astype(jnp.float32) + other1 * w1p[e].astype(jnp.float32)).astype(jnp.bfloat16)

    def stepped(mixed, e):
        return (mixed.astype(jnp.float32) - learn_rate * update[e].astype(jnp.float32)).astype(jnp.bfloat16)

    @pl.loop(0, first_late)
    def _(e):
        nw[e] = mixed_weight(e)

    @pl.loop(0, shards)
    def _(step):
        arrived(update, r_recv, step, 1)
        e = at(step)

        @pl.when(e < first_late)
        def _():
            nw[e] = stepped(nw[e], e)

    @pl.loop(1, shards)
    def _(step):
        send_back(step).wait_send()

    @pl.loop(0, late)
    def _(i):
        send_late(i).wait()
        e = first_late + i
        nw[e] = stepped(mixed_weight(e), e)


def eject_kernel(a, b, c, nt, nw, update, sem):
    copies = [pltpu.make_async_copy(x, o, sem.at[i]) for i, (x, o) in enumerate([(a, nt), (b, nw), (c, update)])]
    for copy in copies:
        copy.start()
    for copy in copies:
        copy.wait()


def local(weight, tracker, grad_new, grad_old, mix_keep):
    shards = lax.axis_size("shard")
    block = weight.shape[1:]
    experts, rows, columns = block
    size = shards * rows
    half = jax.ShapeDtypeStruct(block, jnp.bfloat16)
    full = jax.ShapeDtypeStruct(block, jnp.float32)
    anywhere = pl.BlockSpec(memory_space=pl.ANY)
    scalars = pl.BlockSpec(memory_space=pltpu.SMEM)
    dma = pltpu.SemaphoreType.DMA

    made = pl.pallas_call(
        functools.partial(step_kernel, shards),
        out_shape=(pltpu.VMEM(block, jnp.float32), pltpu.VMEM(block, jnp.bfloat16), pltpu.VMEM(block, jnp.bfloat16)),
        in_specs=[scalars] + [pl.BlockSpec(memory_space=pltpu.HBM)] * 4,
        out_specs=(pl.BlockSpec(memory_space=pltpu.VMEM),) * 3,
        scratch_shapes=[pltpu.VMEM(block, jnp.bfloat16)] * 11
        + [pltpu.VMEM((AHEAD, rows, columns), jnp.bfloat16)] * 2
        + [pltpu.VMEM((size, columns), jnp.bfloat16)] + [pltpu.VMEM((size, size), jnp.bfloat16)] * 2
        + [dma((shards // GROUP,)), dma((shards // SENDS,)), dma((shards // GROUP,)), dma((shards // SENDS,)), dma((shards // GROUP,)), dma((shards // SENDS,)), dma((shards // GROUP,)), dma((shards,)), dma((shards // GROUP,))] + [dma((3,)), dma, dma, dma((4,)), dma((4,))] + [pltpu.SemaphoreType.REGULAR] * 2 + [dma((4,))] + [dma((LATE,))] * 2,
        compiler_params=pltpu.CompilerParams(collective_id=0, has_side_effects=True, vmem_limit_bytes=48 << 20),
        name="step",
    )(mix_keep.T, tracker[0], grad_new[0], grad_old[0], weight[0])
    new_tracker, new_weight, update = pl.pallas_call(
        eject_kernel,
        out_shape=(full, half, half),
        in_specs=[pl.BlockSpec(memory_space=pltpu.VMEM)] * 3,
        out_specs=(pl.BlockSpec(memory_space=pltpu.HBM),) * 3,
        scratch_shapes=[dma((3,))],
        compiler_params=pltpu.CompilerParams(vmem_limit_bytes=1 << 20),
        name="eject",
    )(*made)
    return (new_weight[None], new_tracker[None], update[None])


def solution(mesh):
    spec = P("rep", None, "shard", None)
    return jax.shard_map(
        local,
        mesh=mesh,
        in_specs=(spec, spec, spec, spec, P()),
        out_specs=(spec, spec, spec),
        check_vma=False,
    )
```
